32 devices in a mesh: span: 2 (over x), dom: 16 (over z, y, core).
Axes of the slice: x: 2, y: 2, z: 4, core: 2. Of those that a mesh axis runs over, the one named last changes fastest.
Arguments:
- krylov: float32 [20, 5, 8, 4096], P(None, None, 'span', 'dom'), may hold values from -75 to 75
- limiter: float32 [5, 8, 4096], P(None, 'span', 'dom'), may hold values from 0 to 1
- pseudo_diag: float32 [8, 4096], P('span', 'dom'), may hold values from 1 to 4
- face_states: float32 [2, 5, 8, 8192], P(None, None, 'span', 'dom'), may hold values from -2 to 13.5, as said below
- face_angle: float32 [8192], P('dom'), may hold values from -3.140625 to 3.140625
- face_area: float32 [8192], P('dom'), may hold values from 0.3 to 1.5
- slope_weight: float32 [8192], P('dom'), may hold values from 0.05 to 0.3
- span_coupling: float32 [4096], P('dom'), may hold values from 0.2 to 1
- face_cells: int32 [2, 8192], P(None, 'dom'), may hold values from 0 to 767, as said below
- send_list: int32 [4, 2048], P(None, 'dom'), may hold values from 0 to 255, as said below
- send_count: int32 [4, 16], P(None, 'dom'), may hold values from 0 to 128, as said below
Outputs:
- new_vectors: float32 [3, 5, 8, 4096], P(None, None, 'span', 'dom')
- hessenberg: float32 [3, 23], replicated
The draws below stay inside these ranges and needn't reach their ends.
Inputs may be any that keep to these rules, and one draw needn't show every extreme that they name: `face_cells`: row 0 names owned cells, below 256. A row 1 entry at or above 256 is a ghost slot 256 + j * 128 + k that is live: its sender block exists and k is below that sender's send_count; every live slot of a block is named by exactly one face; a row 1 entry below 256 differs from row 0. `send_list`: entries of one peer slot's list of one block are distinct owned cells. `send_count`: A slot whose receiving block (dom index plus its offset) does not exist has count 0; some block sends a full 128 in slots 2 and 3. `face_states`: each saved state has density and pressure 0.5 or more.
All inputs are finite; a program needn't handle non-finite values.
Results may differ from the reference program's by a relative error of at most 0.00085.
Values sent between devices are 32-bit elements; how exact they have to be, the bound alone decides.
No kernel may reach another device: no remote copies, remote signals or barrier semaphores. Data moves between devices by JAX's collectives and lax.ppermute only.
A program may use at most 64 MiB of HBM per device.

```python
import math
import jax
import jax.numpy as jnp
from jax import lax

K = 20
PRODUCTS = 3
CAP = 128
C = 256
NL = 8
PLANE = 4096
FACES = 8192
N_DOM = 16


OFFSET_LIST = (-2, -1, 1, 2)


def topology(key):
    blocks = PLANE // C
    base = jax.random.fold_in(key, 7103)
    keys_all = jax.random.split(base, 6)
    offsets = jnp.array(OFFSET_LIST, jnp.int32)
    device_ids = jnp.arange(blocks, dtype=jnp.int32)
    targets = device_ids[None, :] + offsets[:, None]
    usable = ((targets >= 0) & (targets < blocks)).astype(jnp.int32)
    counts = jax.random.randint(keys_all[0], (4, blocks), CAP // 8, CAP + 1, dtype=jnp.int32) * usable
    chosen = jax.random.randint(keys_all[1], (), 0, blocks - 2, dtype=jnp.int32)
    counts = counts.at[3, chosen].set(CAP).at[2, chosen].set(CAP)
    list_keys = jax.random.split(keys_all[2], 4 * blocks)
    lists = jax.vmap(lambda one_key: jax.random.permutation(one_key, C)[:CAP])(list_keys)
    lists = lists.reshape(4, blocks, CAP).astype(jnp.int32)
    ramp = jnp.arange(CAP, dtype=jnp.int32)
    lists = lists.at[0, 0].set(C - 1 - ramp).at[1, 0].set(ramp)
    per_dev = 2 * C
    owner_cell = jax.random.randint(keys_all[3], (blocks, per_dev), 0, C, dtype=jnp.int32)
    owner_cell = owner_cell.at[0, 0].set(0)
    interior = (owner_cell + jax.random.randint(keys_all[4], (blocks, per_dev), 1, C, dtype=jnp.int32)) % C
    positions = jnp.arange(per_dev, dtype=jnp.int32)
    peer_slot = jnp.minimum(positions // CAP, 3)
    entry_idx = positions % CAP
    sender = device_ids[:, None] - offsets[peer_slot][None, :]
    clipped = jnp.clip(sender, 0, blocks - 1)
    live_count = counts[peer_slot[None, :], clipped]
    used = (positions[None, :] < 4 * CAP) & (sender >= 0) & (sender < blocks) & (entry_idx[None, :] < live_count)
    other_cell = jnp.where(used, C + positions[None, :], interior).astype(jnp.int32)
    face_pairs = jnp.stack([owner_cell, other_cell]).reshape(2, blocks * per_dev)
    return (face_pairs, lists.reshape(4, blocks * CAP), counts)


def draw_face_cells(key, part):
    return topology(key)[0]


def draw_send_list(key, part):
    return topology(key)[1]


def draw_send_count(key, part):
    return topology(key)[2]


def draw_krylov(key, part):
    keys_all = jax.random.split(jax.random.fold_in(key, 311), 4)
    blocks = PLANE // C
    noise = jax.random.truncated_normal(keys_all[0], -4.0, 4.0, (K, 5, NL, PLANE), jnp.float32)
    shared = jax.random.truncated_normal(keys_all[1], -4.0, 4.0, (5, NL, PLANE), jnp.float32)
    weights = jax.random.uniform(keys_all[2], (K, 1, 1, 1), jnp.float32, 0.5, 1.5)
    rising = 1.0 + 2.0 * (jnp.arange(PLANE) // C).astype(jnp.float32) / max(blocks - 1, 1)
    scales = jnp.ones((1, 5, 1, 1), jnp.float32)
    mixing = 0.6
    return rising * scales * (0.8 * noise + mixing * weights * shared)


def draw_face_states(key, part):
    keys_all = jax.random.split(jax.random.fold_in(key, 523), 5)
    dims = (2, NL, FACES)
    density = jax.random.uniform(keys_all[0], dims, jnp.float32, 0.6, 1.6)
    vel_x = jax.random.uniform(keys_all[1], dims, jnp.float32, 0.2, 2.4)
    pressure = jax.random.uniform(keys_all[4], dims, jnp.float32, 0.6, 2.2)
    vel_y = jnp.clip(0.4 * jax.random.normal(keys_all[2], dims, jnp.float32), -1.0, 1.0)
    vel_z = jnp.clip(0.2 * jax.random.normal(keys_all[3], dims, jnp.float32), -0.5, 0.5)
    energy = pressure / 0.4 + 0.5 * density * (vel_x * vel_x + vel_y * vel_y + vel_z * vel_z)
    return jnp.stack([density, density * vel_x, density * vel_y, density * vel_z, energy], axis=1)


def steps_of(rng, shape, shards, least, top_value):
    loudness, own = 1.0, jax.random.fold_in(rng, 6)
    for dim, shards_of in shards:
        draws = jnp.exp(jax.random.uniform(jax.random.fold_in(own, dim), (shards_of,), jnp.float32, least / len(shards), top_value / len(shards)))
        loudness = loudness * jnp.repeat(draws, shape[dim] // shards_of).reshape([-1 if axis == dim else 1 for axis in range(len(shape))])
    return loudness


def setup_inputs(seed: int = 0) -> dict:
    key_list = jax.random.split(jax.random.key(seed), 12)
    return {
        "krylov": draw_krylov(jax.random.fold_in(key_list[11], 71), 0),
        "limiter": jnp.clip(1.0 * jax.random.uniform(key_list[1], (5, NL, PLANE), jnp.float32) ** steps_of(key_list[1], (5, NL, PLANE), ((1, 2), (2, 16)), -0.2, 0.2), 0.0, 1.0),
        "pseudo_diag": jnp.clip(1.0 + 3.0 * jax.random.uniform(key_list[2], (NL, PLANE), jnp.float32) ** steps_of(key_list[2], (NL, PLANE), ((0, 2), (1, 16)), -0.2, 0.2), 1.0, 4.0),
        "face_states": draw_face_states(jax.random.fold_in(key_list[11], 71), 0),
        "face_angle": jnp.clip(jax.random.uniform(key_list[4], (FACES,), jnp.float32, -3.140625, 3.140625), -3.140625, 3.140625),
        "face_area": jnp.clip(jnp.exp(math.log(1.5) - 1.60943787 * jax.random.uniform(key_list[5], (FACES,), jnp.float32) ** steps_of(key_list[5], (FACES,), ((0, 16),), -0.2, 0.2)), 0.3, 1.5),
        "slope_weight": jnp.clip(jnp.exp(math.log(0.3) - 1.7917595 * jax.random.uniform(key_list[6], (FACES,), jnp.float32) ** steps_of(key_list[6], (FACES,), ((0, 16),), -0.2, 0.2)), 0.05, 0.3),
        "span_coupling": jnp.clip(jnp.exp(math.log(1.0) - 1.609438 * jax.random.uniform(key_list[7], (PLANE,), jnp.float32) ** steps_of(key_list[7], (PLANE,), ((0, 16),), -0.2, 0.2)), 0.2, 1.0),
        "face_cells": draw_face_cells(jax.random.fold_in(key_list[11], 71), 0),
        "send_list": draw_send_list(jax.random.fold_in(key_list[11], 71), 0),
        "send_count": draw_send_count(jax.random.fold_in(key_list[11], 71), 0),
    }


OFFSET_LIST = (-2, -1, 1, 2)
EPSILON = 1e-06

def normal_flux(state_in, normal_x, normal_y):
    density = state_in[0]
    vel_x = state_in[1] / density
    vel_y = state_in[2] / density
    vel_z = state_in[3] / density
    pressure = 0.4 * (state_in[4] - 0.5 * (state_in[1] * vel_x + state_in[2] * vel_y + state_in[3] * vel_z))
    normal_vel = vel_x * normal_x + vel_y * normal_y
    flux_out = jnp.stack([state_in[0] * normal_vel, state_in[1] * normal_vel + pressure * normal_x, state_in[2] * normal_vel + pressure * normal_y, state_in[3] * normal_vel, (state_in[4] + pressure) * normal_vel])
    wave_speed = jnp.abs(normal_vel) + jnp.sqrt(1.4 * pressure / density)
    return (flux_out, wave_speed)

def face_flux(left_state, right_state, normal_x, normal_y, face_area):
    flux_left, speed_left = normal_flux(left_state, normal_x, normal_y)
    flux_right, speed_right = normal_flux(right_state, normal_x, normal_y)
    wave_bound = lax.stop_gradient(jnp.maximum(speed_left, speed_right))
    return face_area * (0.5 * (flux_left + flux_right) - 0.5 * wave_bound * (right_state - left_state))

def flux_transpose(states, normal_x, normal_y, face_area, cotangent):

    def applied(left_in, right_in):
        return face_flux(left_in, right_in, normal_x, normal_y, face_area)
    _, pullback = jax.vjp(applied, states[0], states[1])
    return pullback(cotangent)

def prepare(face_cells, send_list, send_count):
    per_dev = 2 * C
    face_total = face_cells.shape[1]
    device = jnp.arange(face_total, dtype=jnp.int32) // per_dev
    owner_cell = device * C + face_cells[0]
    local_idx = face_cells[1]
    ghost_slot = jnp.maximum(local_idx - C, 0)
    peer_slot = jnp.minimum(ghost_slot // CAP, 3)
    entry_idx = ghost_slot % CAP
    offsets = jnp.array(OFFSET_LIST, jnp.int32)
    sender = device - offsets[peer_slot]
    clipped = jnp.clip(sender, 0, N_DOM - 1)
    live = (sender >= 0) & (sender < N_DOM) & (entry_idx < send_count[peer_slot, clipped])
    remote = clipped * C + send_list[peer_slot, clipped * CAP + entry_idx]
    is_local = local_idx < C
    other_cell = jnp.where(is_local, device * C + local_idx, remote).astype(jnp.int32)
    live_weight = jnp.where(is_local | live, 1.0, 0.0).astype(jnp.float32)
    return (owner_cell.astype(jnp.int32), other_cell, live_weight)

def transposed_apply(vector, limiter, pseudo_diag, face_states, normal_x, normal_y, face_area, slope_weight, span_coupling, owner_cell, other_cell, live_weight):

    def layer_terms(inputs):
        values, states, limits = inputs
        jump_vals = values[:, owner_cell] - live_weight * values[:, other_cell]
        adj_left, adj_right = flux_transpose(states, normal_x, normal_y, face_area, jump_vals)
        state_part = jnp.zeros(values.shape, jnp.float32).at[:, owner_cell].add(adj_left)
        state_part = state_part.at[:, other_cell].add(live_weight * adj_right)
        slope_adj = limits * state_part
        moved = slope_weight * (slope_adj[:, owner_cell] - live_weight * slope_adj[:, other_cell])
        slope_part = jnp.zeros(values.shape, jnp.float32).at[:, owner_cell].add(-moved)
        slope_part = slope_part.at[:, other_cell].add(live_weight * moved)
        return state_part + slope_part
    stacked = lax.map(layer_terms, (jnp.moveaxis(vector, 1, 0), jnp.moveaxis(face_states, 2, 0), jnp.moveaxis(limiter, 1, 0)))
    face_terms = jnp.moveaxis(stacked, 0, 1)
    spanwise = span_coupling * (2.0 * vector - jnp.roll(vector, 1, axis=1) - jnp.roll(vector, -1, axis=1))
    return pseudo_diag * vector + spanwise + face_terms

def reference(krylov, limiter, pseudo_diag, face_states, face_angle, face_area, slope_weight, span_coupling, face_cells, send_list, send_count):
    dense_reference = lax.Precision.HIGHEST
    owner_cell, other_cell, live_weight = prepare(face_cells, send_list, send_count)
    normal_x = jnp.cos(face_angle)
    normal_y = jnp.sin(face_angle)
    count_all = 5 * NL * PLANE
    krylov_dimension = krylov.shape[0]
    gram = jnp.einsum('kvlc,jvlc->kj', krylov, krylov, precision=dense_reference) / count_all
    factor = jnp.linalg.cholesky(gram)
    vectors = []
    hess_rows = []
    current = krylov[krylov_dimension - 1]
    for number in range(PRODUCTS):
        adjoint_output = transposed_apply(current, limiter, pseudo_diag, face_states, normal_x, normal_y, face_area, slope_weight, span_coupling, owner_cell, other_cell, live_weight)
        partition_sums = jnp.einsum('zbis,bis->z', krylov, adjoint_output, precision=dense_reference)
        if vectors:
            extra_sums = jnp.stack([jnp.sum(finished * adjoint_output) for finished in vectors])
            partition_sums = jnp.concatenate([partition_sums, extra_sums])
        projected_vector = partition_sums / count_all
        solved = jax.scipy.linalg.cho_solve((factor, True), projected_vector[:krylov_dimension])
        hessenberg_column = jnp.concatenate([solved, projected_vector[krylov_dimension:]])
        residual_piece = adjoint_output - jnp.einsum('p,pohz->ohz', hessenberg_column[:krylov_dimension], krylov, precision=dense_reference)
        for position, finished in enumerate(vectors):
            residual_piece = residual_piece - hessenberg_column[krylov_dimension + position] * finished
        scale_norm = jnp.sqrt(jnp.sum(residual_piece * residual_piece) / count_all + EPSILON)
        current = residual_piece / scale_norm
        vectors.append(current)
        hess_rows.append(jnp.concatenate([hessenberg_column, jnp.zeros((krylov_dimension + PRODUCTS - 1 - hessenberg_column.shape[0],), jnp.float32), jnp.reshape(scale_norm, (1,))]))
    return (jnp.stack(vectors), jnp.stack(hess_rows))
```

```python
import functools

import jax
import jax.numpy as jnp
from jax import lax
from jax.experimental import pallas as pl
from jax.experimental.pallas import tpu as pltpu
from jax.sharding import PartitionSpec as P

PRODUCTS = 3
PEERS = 4
EPSILON = 1e-06
GAMMA = 1.4
LANES = 128
DOT_LANES = 28

PIECE_OF_SENDER = (4, 1, 3, 2)
PIECE_OF_HOLDER = (2, 3, 1, 4)

VMEM_LIMIT = 16 * 1024 * 1024
NT = (((1,), (1,)), ((), ()))


def call(kernel, out_shape, *args, smem=(), scratch=()):
    specs = [
        pl.BlockSpec(memory_space=pltpu.SMEM if i in smem else pltpu.VMEM)
        for i in range(len(args))
    ]
    out_specs = jax.tree.map(lambda _: pl.BlockSpec(memory_space=pltpu.VMEM), out_shape)
    return pl.pallas_call(
        kernel,
        out_shape=out_shape,
        in_specs=specs,
        out_specs=out_specs,
        scratch_shapes=list(scratch),
        compiler_params=pltpu.CompilerParams(vmem_limit_bytes=VMEM_LIMIT),
    )(*args)


def f32(*shape):
    return jax.ShapeDtypeStruct(shape, jnp.float32)


def i32(*shape):
    return jax.ShapeDtypeStruct(shape, jnp.int32)


def split_rows(value):
    high = value.astype(jnp.bfloat16).astype(jnp.float32)
    return jnp.concatenate([high, value - high], axis=0).astype(jnp.bfloat16)


def primitives(states_ref, side, nx, ny):
    rho = states_ref[side, 0]
    inverse = 1.0 / rho
    ux = states_ref[side, 1] * inverse
    uy = states_ref[side, 2] * inverse
    uz = states_ref[side, 3] * inverse
    energy = states_ref[side, 4]
    pressure = (GAMMA - 1.0) * (energy - 0.5 * rho * (ux * ux + uy * uy + uz * uz))
    enthalpy = (energy + pressure) * inverse
    speed = jnp.abs(ux * nx + uy * ny) + jnp.sqrt(GAMMA * pressure * inverse)
    return [ux, uy, uz, enthalpy], speed


def prepare_kernel(cells, cap, bits, odd_ref, states_ref, nx_ref, ny_ref, area_ref, slope_ref,
                   face_cells_ref, list_ref, coef_ref, row_ref, index_ref, message_ref):
    faces = nx_ref.shape[1]
    layers = states_ref.shape[2]
    nx, ny = nx_ref[...], ny_ref[...]
    half = 0.5 * area_ref[...]
    left, speed_left = primitives(states_ref, 0, nx, ny)
    right, speed_right = primitives(states_ref, 1, nx, ny)
    bound = half * jnp.maximum(speed_left, speed_right)
    for k, value in enumerate(left + right + [bound]):
        coef_ref[k] = value
    rows = [half * nx, half * ny, slope_ref[...]]
    for k, value in enumerate(rows):
        row_ref[k : k + 1, :] = value

    is_odd = odd_ref[0] == 1
    owner = face_cells_ref[0:1, :]
    other = face_cells_ref[1:2, :]
    lists = [
        jnp.where(is_odd, list_ref[PEERS - 1 - g : PEERS - g, :], list_ref[g : g + 1, :])
        for g in range(PEERS)
    ]
    ghost = other - cells
    group = jnp.zeros_like(ghost)
    for g in range(1, PEERS):
        group = group + (ghost >= g * cap).astype(jnp.int32)
    mirrored = ghost + (PEERS - 1 - 2 * group) * cap
    slot = jnp.where(jnp.logical_and(is_odd, ghost >= 0), mirrored, ghost)
    index_ref[0:1, :] = owner
    index_ref[1:2, :] = slot + cells
    for g in range(PEERS):
        index_ref[2:3, g * cap : (g + 1) * cap] = lists[g]

    packed = jnp.concatenate(right + [bound] + rows + [owner.astype(jnp.float32)], axis=0)
    count = packed.shape[0]
    named = lax.broadcasted_iota(jnp.int32, (PEERS * cap, faces), 0) == slot
    picked = lax.dot_general(
        split_rows(packed), named.astype(jnp.float32).astype(jnp.bfloat16), NT,
        preferred_element_type=jnp.float32,
    )
    picked = picked[:count] + picked[count:]
    for g in range(PEERS):
        part = picked[:, g * cap : (g + 1) * cap]
        code = part[count - 1 :] * float(1 << bits) + lists[PEERS - 1 - g].astype(jnp.float32)
        message_ref[g * count : (g + 1) * count - 1, :] = part[: count - 1]
        message_ref[(g + 1) * count - 1 : (g + 1) * count, :] = code


def build_kernel(cells, cap, bits, layers, coef_ref, row_ref, index_ref, m0, m1, m2, m3,
                 flux_ref, where_ref, hot_ref):
    messages = (m0, m1, m2, m3)
    faces = coef_ref.shape[2]
    last = m0.shape[0] - 1
    zeros = jnp.zeros((layers, faces), jnp.float32)

    def across(row):
        return jnp.concatenate([m[row : row + 1, :] for m in messages], axis=1)

    def block(k):
        return jnp.concatenate([m[k * layers : (k + 1) * layers, :] for m in messages], axis=1)

    def twice(own, cut):
        return jnp.concatenate(
            [jnp.broadcast_to(own, (layers, faces)), jnp.broadcast_to(cut, (layers, faces))], axis=0
        )

    left = [jnp.concatenate([coef_ref[k], zeros], axis=0) for k in range(4)]
    right = [jnp.concatenate([coef_ref[4 + k], block(k)], axis=0) for k in range(4)]
    bound = jnp.concatenate([coef_ref[8], block(4)], axis=0)
    nx, ny, slope = [twice(row_ref[k : k + 1, :], across(5 * layers + k)) for k in range(3)]
    values = []
    for ux, uy, uz, enthalpy in (left, right):
        values += [ux, uy, uz, enthalpy, ux * nx + uy * ny, 0.5 * (ux * ux + uy * uy + uz * uz)]
    for k, value in enumerate(values + [bound, nx, ny, slope]):
        flux_ref[k] = value

    code = [m[last : last + 1, :].astype(jnp.int32) for m in messages]
    held = jnp.concatenate([lax.shift_right_logical(c, bits) for c in code], axis=1)
    sent = [jnp.bitwise_and(code[PEERS - 1 - g], (1 << bits) - 1) for g in range(PEERS)]
    owner, other, mine = index_ref[0:1, :], index_ref[1:2, :], index_ref[2:3, :]
    ghost = other - cells
    table = [
        jnp.broadcast_to(sent[g] + PIECE_OF_SENDER[g] * cells, (2 * layers, cap)) for g in range(PEERS)
    ]
    found = []
    for f in range(faces // LANES):
        slot = jnp.broadcast_to(ghost[:, f * LANES : (f + 1) * LANES], (2 * layers, LANES))
        low = jnp.bitwise_and(slot, LANES - 1)
        value = jnp.broadcast_to(other[:, f * LANES : (f + 1) * LANES], (2 * layers, LANES))
        for g in range(PEERS):
            picked = jnp.take_along_axis(table[g], low, axis=1, mode="promise_in_bounds")
            inside = jnp.logical_and(slot >= g * cap, slot < (g + 1) * cap)
            value = jnp.where(inside, picked, value)
        found.append(value[0:1])
    far = jnp.concatenate(found, axis=1)
    where_ref[0] = twice(owner, held)
    where_ref[1] = twice(far, mine)
    cell = lax.broadcasted_iota(jnp.int32, (cells, faces), 0)
    used = slope[layers : layers + 1, :] != 0.0
    one = jnp.float32(1.0)
    hot_ref[0] = jnp.where(cell == owner, one, 0.0).astype(jnp.bfloat16)
    hot_ref[1] = jnp.where(cell == other, one, 0.0).astype(jnp.bfloat16)
    hot_ref[2] = jnp.where(cell == jnp.where(used, mine, -1), one, 0.0).astype(jnp.bfloat16)


def gather_jump(pieces, where_ref, layers, tiles, variables, f):
    rows = 2 * layers
    upper = lax.broadcasted_iota(jnp.int32, (rows, LANES), 0) < layers
    near = where_ref[0, :, f * LANES : (f + 1) * LANES]
    far = where_ref[1, :, f * LANES : (f + 1) * LANES]
    near_low, near_tile = jnp.bitwise_and(near, LANES - 1), lax.shift_right_logical(near, 7)
    far_low, far_tile = jnp.bitwise_and(far, LANES - 1), lax.shift_right_logical(far, 7)
    holder = PIECE_OF_HOLDER[f]

    def take(source, index):
        return jnp.take_along_axis(source, index, axis=1, mode="promise_in_bounds")

    jumps = []
    for v in range(variables):
        value = None
        for t in range(tiles):
            source = jnp.where(upper, pieces[0][v][t], pieces[holder][v][t])
            got = take(source, near_low)
            value = got if value is None else jnp.where(near_tile == t, got, value)
        other = None
        for p in range(len(pieces)):
            for t in range(tiles):
                got = take(pieces[p][v][t], far_low)
                other = got if other is None else jnp.where(far_tile == p * tiles + t, got, other)
        jumps.append(value - other)
    return jumps


def doubled(refs, layers, tiles, variables):
    rows = layers * tiles
    pieces = []
    for ref, base in refs:
        piece = []
        for v in range(variables):
            parts = []
            for t in range(tiles):
                start = base + v * rows + t * layers
                part = ref[start : start + layers, :]
                parts.append(jnp.concatenate([part, part], axis=0))
            piece.append(parts)
        pieces.append(piece)
    return pieces


def side_flux(coefs, nx, ny, e):
    ux, uy, uz, enthalpy, normal, kinetic = coefs
    alpha = ux * e[1] + uy * e[2] + uz * e[3] + enthalpy * e[4]
    beta = (GAMMA - 1.0) * (nx * e[1] + ny * e[2] + normal * e[4])
    total = e[0] + alpha
    return [
        beta * kinetic - alpha * normal,
        nx * total + normal * e[1] - beta * ux,
        ny * total + normal * e[2] - beta * uy,
        normal * e[3] - beta * uz,
        beta + normal * e[4],
    ]


def scatter(value, hot_ref, k):
    got = lax.dot_general(split_rows(value), hot_ref[k], NT, preferred_element_type=jnp.float32)
    half = got.shape[0] // 2
    return got[:half] + got[half:]


def to_tiles(value, tiles):
    return jnp.concatenate([value[:, t * LANES : (t + 1) * LANES] for t in range(tiles)], axis=0)


def state_kernel(layers, tiles, variables, bases, x_ref, a_ref, b_ref, c_ref, flux_ref, where_ref,
                 hot_ref, limiter_ref, p_ref, s_ref, left_ref, right_ref):
    rows = layers * tiles
    size = variables * rows
    refs = ((x_ref, bases[0]), (a_ref, bases[1]), (b_ref, bases[2]), (b_ref, bases[2] + size), (c_ref, bases[3]))
    pieces = doubled(refs, layers, tiles, variables)
    faces = flux_ref.shape[2]
    for f in range(faces // LANES):
        lanes = slice(f * LANES, (f + 1) * LANES)
        e = gather_jump(pieces, where_ref, layers, tiles, variables, f)
        coefs = [flux_ref[k, :, lanes] for k in range(15)]
        bound, nx, ny = coefs[12:]
        left = side_flux(coefs[0:6], nx, ny, e)
        right = side_flux(coefs[6:12], nx, ny, e)
        for v in range(variables):
            left_ref[v * 2 * layers : (v + 1) * 2 * layers, lanes] = left[v] + bound * e[v]
            right_ref[v * 2 * layers : (v + 1) * 2 * layers, lanes] = right[v] - bound * e[v]
    left, right = left_ref[...], right_ref[...]
    near = scatter(left, hot_ref, 0) + scatter(right, hot_ref, 1)
    cut = scatter(right, hot_ref, 2)
    for v in range(variables):
        at = v * 2 * layers
        part = to_tiles(near[at : at + layers] + cut[at + layers : at + 2 * layers], tiles)
        p_ref[v * rows : (v + 1) * rows, :] = part
        s_ref[v * rows : (v + 1) * rows, :] = part * limiter_ref[v * rows : (v + 1) * rows, :]


def slope_kernel(layers, tiles, variables, vectors, with_gram, x_ref, a_ref, b_ref, c_ref, flux_ref,
                 where_ref, hot_ref, p_ref, v_ref, low_ref, high_ref, diag_ref, couple_ref, krylov_ref, *rest):
    finished = rest[:vectors]
    rest = rest[vectors:]
    if with_gram:
        gram_ref, *rest = rest
    w_ref, dots_ref, moved_ref, sums_ref = rest
    rows = layers * tiles
    size = variables * rows
    refs = ((x_ref, 0), (a_ref, 0), (b_ref, 0), (b_ref, size), (c_ref, 0))
    pieces = doubled(refs, layers, tiles, variables)
    faces = flux_ref.shape[2]
    for f in range(faces // LANES):
        lanes = slice(f * LANES, (f + 1) * LANES)
        e = gather_jump(pieces, where_ref, layers, tiles, variables, f)
        slope = flux_ref[15, :, lanes]
        for v in range(variables):
            moved_ref[v * 2 * layers : (v + 1) * 2 * layers, lanes] = slope * e[v]
    moved = moved_ref[...]
    own = scatter(moved, hot_ref, 1) - scatter(moved, hot_ref, 0)
    cut = scatter(moved, hot_ref, 2)
    layer = lax.broadcasted_iota(jnp.int32, (rows, LANES), 0) % layers
    total = []
    for v in range(variables):
        at = v * 2 * layers
        part = slice(v * rows, (v + 1) * rows)
        slope_part = to_tiles(own[at : at + layers] + cut[at + layers : at + 2 * layers], tiles)
        value = v_ref[part, :]
        low = pltpu.roll(low_ref[part, :], rows - (layers - 1), axis=0)
        high = pltpu.roll(high_ref[part, :], layers - 1, axis=0)
        above = jnp.where(layer == layers - 1, high, pltpu.roll(value, rows - 1, axis=0))
        below = jnp.where(layer == 0, low, pltpu.roll(value, 1, axis=0))
        out = diag_ref[...] * value + couple_ref[...] * (2.0 * value - above - below)
        out = out + p_ref[part, :] + slope_part
        w_ref[part, :] = out
        total.append(out)
    sums_ref[...] = jnp.zeros_like(sums_ref)
    basis = krylov_ref.shape[0] // size

    def put(at, ref, base):
        acc = None
        for v in range(variables):
            term = ref[base + v * rows : base + (v + 1) * rows, :] * total[v]
            acc = term if acc is None else acc + term
        sums_ref[at : at + 1, :] = jnp.sum(acc, axis=0, keepdims=True)

    for i in range(basis):
        put(i, krylov_ref, i * size)
    for j in range(vectors):
        put(basis + j, finished[j], 0)
    put(basis + PRODUCTS, w_ref, 0)
    dots = lax.dot_general(
        jnp.ones((8, LANES), jnp.float32), sums_ref[...], NT,
        precision=lax.Precision.HIGHEST, preferred_element_type=jnp.float32,
    )
    if with_gram:
        message = gram_ref[...]
        message = jnp.concatenate([message[0:1] + dots[0:1], message[1:]], axis=0)
        dots_ref[...] = jnp.broadcast_to(message[None], dots_ref.shape)
    else:
        dots_ref[...] = jnp.broadcast_to(dots[0:1], dots_ref.shape)


def inverse_of(packed, basis, per_row, scratch_ref):
    height = scratch_ref.shape[0]
    lane = lax.broadcasted_iota(jnp.int32, (height, LANES), 1)
    row = lax.broadcasted_iota(jnp.int32, (height, LANES), 0)
    scratch_ref[...] = jnp.zeros_like(scratch_ref)
    for i in range(basis):
        at = DOT_LANES + (i % per_row) * basis
        scratch_ref[i : i + 1, 0:basis] = packed[i // per_row : i // per_row + 1, at : at + basis]
    work = scratch_ref[...] + jnp.where(jnp.logical_and(lane == row + basis, row < basis), 1.0, 0.0)
    for k in range(basis):
        pivot_row = work[k : k + 1, :]
        scaled = pivot_row / pivot_row[:, k : k + 1]
        column = jnp.where(row == k, 0.0, jnp.broadcast_to(work[:, k : k + 1], work.shape))
        work = jnp.where(row == k, scaled, work - column * scaled)
    moved = pltpu.roll(work, LANES - basis, axis=1)
    return jnp.where(lane < basis, moved, 0.0)


def update_kernel(count_all, size, vectors, with_gram, per_row, got_ref, w_ref, krylov_ref, *rest):
    finished = rest[:vectors]
    rest = rest[vectors:]
    if with_gram:
        next_ref, hess_ref, inverse_ref, scratch_ref = rest
    else:
        inverse_ref, next_ref, hess_ref = rest
    basis = krylov_ref.shape[0] // size
    scale = 1.0 / count_all
    if with_gram:
        packed = jnp.sum(got_ref[...], axis=0) * scale
        inverse = inverse_of(packed, basis, per_row, scratch_ref)
        inverse_ref[...] = inverse
        p = packed[0:1, :]
    else:
        p = jnp.sum(got_ref[...], axis=0, keepdims=True) * scale
        inverse = inverse_ref[...]
    lane = lax.broadcasted_iota(jnp.int32, (1, LANES), 1)
    square = jnp.sum(jnp.where(lane == basis + PRODUCTS, p, 0.0), axis=1, keepdims=True)
    wide = inverse.shape
    solved = jnp.broadcast_to(jnp.sum(inverse * p, axis=1, keepdims=True), wide)
    diagonal = lax.broadcasted_iota(jnp.int32, wide, 0) == lax.broadcasted_iota(jnp.int32, wide, 1)
    solved_row = jnp.sum(jnp.where(diagonal, solved, 0.0), axis=0, keepdims=True)
    column = jnp.where(lane < basis, solved_row, jnp.where(lane < basis + vectors, p, 0.0))
    norm = jnp.sqrt(square - jnp.sum(column * p, axis=1, keepdims=True) + EPSILON)
    hess_ref[...] = jnp.where(lane == basis + PRODUCTS - 1, norm, column)
    rest_of = w_ref[...]
    for i in range(basis):
        rest_of = rest_of - solved[i : i + 1, :] * krylov_ref[i * size : (i + 1) * size, :]
    for j in range(vectors):
        rest_of = rest_of - p[:, basis + j : basis + j + 1] * finished[j][...]
    next_ref[...] = rest_of / norm


def on_device(krylov, limiter, pseudo_diag, face_states, face_angle, face_area, slope_weight,
              span_coupling, face_cells, send_list, send_count):
    basis, variables, layers, cells = krylov.shape
    cap = send_list.shape[1]
    faces = face_cells.shape[1]
    tiles = cells // LANES
    rows = layers * tiles
    size = variables * rows
    dom_count = lax.axis_size("dom")
    span_count = lax.axis_size("span")
    devices = dom_count * span_count
    count_all = variables * layers * cells * devices
    bits = (cells - 1).bit_length()
    messages = 5 * layers + 4
    height = -(-basis // 8) * 8
    per_row = (LANES - DOT_LANES) // basis
    packed_rows = -(-basis // per_row)

    def in_rows(value):
        lead = value.shape[:-2]
        value = value.reshape(lead + (layers, tiles, LANES))
        return jnp.swapaxes(value, -3, -2).reshape(lead[:-1] + (-1, LANES) if lead else (rows, LANES))

    swap = [(i, i ^ 1) for i in range(dom_count)]
    hop = [(i, i + 2 - 4 * (i % 2)) for i in range(dom_count) if 0 <= i + 2 - 4 * (i % 2) < dom_count]

    def window(x):
        a = lax.ppermute(x, "dom", swap)
        b = lax.ppermute(jnp.concatenate([x, a], axis=0), "dom", hop)
        c = lax.ppermute(b[size:], "dom", swap)
        return a, b, c

    def layer_neighbours(x):
        up = [(i, (i + 1) % span_count) for i in range(span_count)]
        low = lax.ppermute(x, "span", up)
        if span_count == 2:
            return low, low
        return low, lax.ppermute(x, "span", [(t, s) for s, t in up])

    odd = (lax.axis_index("dom") % 2).astype(jnp.int32).reshape(1)
    as_row = lambda value: value.reshape(1, faces)
    coef, row, index, message = call(
        functools.partial(prepare_kernel, cells, cap, bits),
        (f32(9, layers, faces), f32(3, faces), i32(3, faces), f32(PEERS * messages, cap)),
        odd, face_states, as_row(jnp.cos(face_angle)), as_row(jnp.sin(face_angle)),
        as_row(face_area), as_row(slope_weight), face_cells, send_list, smem=(0,),
    )
    basis_rows = in_rows(krylov.reshape(basis * variables, layers, cells)).reshape(basis * size, LANES)
    current = basis_rows[(basis - 1) * size :]
    first = jnp.concatenate([current, message[messages:]], axis=0)
    a = lax.ppermute(first, "dom", swap)
    second = jnp.concatenate(
        [current, a[:size], message[:messages], a[size + messages :]], axis=0
    )
    b = lax.ppermute(second, "dom", hop)
    third = jnp.concatenate([b[size : 2 * size], b[2 * size + 2 * messages :]], axis=0)
    c = lax.ppermute(third, "dom", swap)
    window_now = (a, b, c)

    flux, where, hot = call(
        functools.partial(build_kernel, cells, cap, bits, layers),
        (
            f32(16, 2 * layers, faces),
            i32(2, 2 * layers, faces),
            jax.ShapeDtypeStruct((3, cells, faces), jnp.bfloat16),
        ),
        coef, row, index,
        b[2 * size : 2 * size + messages],
        b[2 * size + messages : 2 * size + 2 * messages],
        a[size : size + messages],
        c[size:],
    )

    gram = jnp.einsum("kvlc,jvlc->kj", krylov, krylov, precision=lax.Precision.HIGHEST)
    gram = jnp.pad(gram, ((0, packed_rows * per_row - basis), (0, 0)))
    gram = gram.reshape(packed_rows, per_row * basis)
    gram = jnp.pad(gram, ((0, 0), (DOT_LANES, LANES - DOT_LANES - per_row * basis)))
    limit_rows = in_rows(limiter)
    diag_rows = in_rows(pseudo_diag)
    couple_rows = jnp.repeat(span_coupling.reshape(tiles, LANES), layers, axis=0)

    vectors = []
    hess_rows = []
    inverse = None
    for number in range(PRODUCTS):
        low, high = layer_neighbours(current)
        state_part, slope_adj = call(
            functools.partial(state_kernel, layers, tiles, variables, (0, 0, 0, 0)),
            (f32(size, LANES), f32(size, LANES)),
            current, *window_now, flux, where, hot, limit_rows,
            scratch=[pltpu.VMEM((variables * 2 * layers, faces), jnp.float32)] * 2,
        )
        slope_window = window(slope_adj)
        with_gram = number == 0
        extra = [gram] if with_gram else []
        dots_shape = f32(devices, packed_rows, LANES) if with_gram else f32(devices, LANES)
        product, dots = call(
            functools.partial(slope_kernel, layers, tiles, variables, number, with_gram),
            (f32(size, LANES), dots_shape),
            slope_adj, *slope_window, flux, where, hot, state_part, current, low, high, diag_rows,
            couple_rows, basis_rows, *vectors, *extra,
            scratch=[
                pltpu.VMEM((variables * 2 * layers, faces), jnp.float32),
                pltpu.VMEM((LANES, LANES), jnp.float32),
            ],
        )
        got = lax.all_to_all(dots, ("span", "dom"), 0, 0, tiled=True)
        next_shapes = (f32(size, LANES), f32(1, LANES))
        update = functools.partial(update_kernel, count_all, size, number, with_gram, per_row)
        if with_gram:
            current, hess, inverse = call(
                update, next_shapes + (f32(height, LANES),), got, product, basis_rows,
                scratch=[pltpu.VMEM((height, LANES), jnp.float32)],
            )
        else:
            current, hess = call(update, next_shapes, got, product, basis_rows, *vectors, inverse)
        vectors.append(current)
        hess_rows.append(hess[:, : basis + PRODUCTS])
        if number + 1 < PRODUCTS:
            window_now = window(current)
    stacked = jnp.stack(vectors).reshape(PRODUCTS, variables, tiles, layers, LANES)
    stacked = jnp.swapaxes(stacked, 2, 3).reshape(PRODUCTS, variables, layers, cells)
    return (stacked, jnp.concatenate(hess_rows, axis=0))


def solution(mesh):
    return jax.shard_map(
        on_device,
        mesh=mesh,
        in_specs=(
            P(None, None, "span", "dom"),
            P(None, "span", "dom"),
            P("span", "dom"),
            P(None, None, "span", "dom"),
            P("dom"),
            P("dom"),
            P("dom"),
            P("dom"),
            P(None, "dom"),
            P(None, "dom"),
            P(None, "dom"),
        ),
        out_specs=(P(None, None, "span", "dom"), P()),
        check_vma=False,
    )
```

```python
import functools

import jax
import jax.numpy as jnp
from jax import lax
from jax.experimental import pallas as pl
from jax.experimental.pallas import tpu as pltpu
from jax.sharding import PartitionSpec as P

PRODUCTS = 3
PEERS = 4
EPSILON = 1e-06
GAMMA = 1.4
LANES = 128
DOT_LANES = 28

PIECE_OF_SENDER = (4, 1, 3, 2)
PIECE_OF_HOLDER = (2, 3, 1, 4)

VMEM_LIMIT = 16 * 1024 * 1024
NT = (((1,), (1,)), ((), ()))


def call(kernel, out_shape, *args, smem=(), scratch=()):
    specs = [
        pl.BlockSpec(memory_space=pltpu.SMEM if i in smem else pltpu.VMEM)
        for i in range(len(args))
    ]
    out_specs = jax.tree.map(lambda _: pl.BlockSpec(memory_space=pltpu.VMEM), out_shape)
    return pl.pallas_call(
        kernel,
        out_shape=out_shape,
        in_specs=specs,
        out_specs=out_specs,
        scratch_shapes=list(scratch),
        compiler_params=pltpu.CompilerParams(vmem_limit_bytes=VMEM_LIMIT),
    )(*args)


def f32(*shape):
    return jax.ShapeDtypeStruct(shape, jnp.float32)


def i32(*shape):
    return jax.ShapeDtypeStruct(shape, jnp.int32)


def split_rows(value):
    high = value.astype(jnp.bfloat16).astype(jnp.float32)
    return jnp.concatenate([high, value - high], axis=0).astype(jnp.bfloat16)


def primitives(states_ref, side, nx, ny):
    rho = states_ref[side, 0]
    inverse = 1.0 / rho
    ux = states_ref[side, 1] * inverse
    uy = states_ref[side, 2] * inverse
    uz = states_ref[side, 3] * inverse
    energy = states_ref[side, 4]
    pressure = (GAMMA - 1.0) * (energy - 0.5 * rho * (ux * ux + uy * uy + uz * uz))
    enthalpy = (energy + pressure) * inverse
    speed = jnp.abs(ux * nx + uy * ny) + jnp.sqrt(GAMMA * pressure * inverse)
    return [ux, uy, uz, enthalpy], speed


def prepare_kernel(cells, cap, bits, odd_ref, states_ref, nx_ref, ny_ref, area_ref, slope_ref,
                   face_cells_ref, list_ref, coef_ref, row_ref, index_ref, message_ref):
    faces = nx_ref.shape[1]
    layers = states_ref.shape[2]
    nx, ny = nx_ref[...], ny_ref[...]
    half = 0.5 * area_ref[...]
    left, speed_left = primitives(states_ref, 0, nx, ny)
    right, speed_right = primitives(states_ref, 1, nx, ny)
    bound = half * jnp.maximum(speed_left, speed_right)
    for k, value in enumerate(left + right + [bound]):
        coef_ref[k] = value
    rows = [half * nx, half * ny, slope_ref[...]]
    for k, value in enumerate(rows):
        row_ref[k : k + 1, :] = value

    is_odd = odd_ref[0] == 1
    owner = face_cells_ref[0:1, :]
    other = face_cells_ref[1:2, :]
    lists = [
        jnp.where(is_odd, list_ref[PEERS - 1 - g : PEERS - g, :], list_ref[g : g + 1, :])
        for g in range(PEERS)
    ]
    ghost = other - cells
    group = jnp.zeros_like(ghost)
    for g in range(1, PEERS):
        group = group + (ghost >= g * cap).astype(jnp.int32)
    mirrored = ghost + (PEERS - 1 - 2 * group) * cap
    slot = jnp.where(jnp.logical_and(is_odd, ghost >= 0), mirrored, ghost)
    index_ref[0:1, :] = owner
    index_ref[1:2, :] = slot + cells
    for g in range(PEERS):
        index_ref[2:3, g * cap : (g + 1) * cap] = lists[g]

    packed = jnp.concatenate(right + [bound] + rows + [owner.astype(jnp.float32)], axis=0)
    count = packed.shape[0]
    named = lax.broadcasted_iota(jnp.int32, (PEERS * cap, faces), 0) == slot
    picked = lax.dot_general(
        split_rows(packed), named.astype(jnp.float32).astype(jnp.bfloat16), NT,
        preferred_element_type=jnp.float32,
    )
    picked = picked[:count] + picked[count:]
    for g in range(PEERS):
        part = picked[:, g * cap : (g + 1) * cap]
        code = part[count - 1 :] * float(1 << bits) + lists[PEERS - 1 - g].astype(jnp.float32)
        message_ref[g * count : (g + 1) * count - 1, :] = part[: count - 1]
        message_ref[(g + 1) * count - 1 : (g + 1) * count, :] = code


def build_kernel(cells, cap, bits, layers, coef_ref, row_ref, index_ref, m0, m1, m2, m3,
                 flux_ref, where_ref, hot_ref):
    messages = (m0, m1, m2, m3)
    faces = coef_ref.shape[2]
    last = m0.shape[0] - 1
    zeros = jnp.zeros((layers, faces), jnp.float32)

    def across(row):
        return jnp.concatenate([m[row : row + 1, :] for m in messages], axis=1)

    def block(k):
        return jnp.concatenate([m[k * layers : (k + 1) * layers, :] for m in messages], axis=1)

    def twice(own, cut):
        return jnp.concatenate(
            [jnp.broadcast_to(own, (layers, faces)), jnp.broadcast_to(cut, (layers, faces))], axis=0
        )

    left = [jnp.concatenate([coef_ref[k], zeros], axis=0) for k in range(4)]
    right = [jnp.concatenate([coef_ref[4 + k], block(k)], axis=0) for k in range(4)]
    bound = jnp.concatenate([coef_ref[8], block(4)], axis=0)
    nx, ny, slope = [twice(row_ref[k : k + 1, :], across(5 * layers + k)) for k in range(3)]
    values = []
    for ux, uy, uz, enthalpy in (left, right):
        values += [ux, uy, uz, enthalpy, ux * nx + uy * ny, 0.5 * (ux * ux + uy * uy + uz * uz)]
    for k, value in enumerate(values + [bound, nx, ny, slope]):
        flux_ref[k] = value

    code = [m[last : last + 1, :].astype(jnp.int32) for m in messages]
    held = jnp.concatenate([lax.shift_right_logical(c, bits) for c in code], axis=1)
    sent = [jnp.bitwise_and(code[PEERS - 1 - g], (1 << bits) - 1) for g in range(PEERS)]
    owner, other, mine = index_ref[0:1, :], index_ref[1:2, :], index_ref[2:3, :]
    ghost = other - cells
    table = [
        jnp.broadcast_to(sent[g] + PIECE_OF_SENDER[g] * cells, (2 * layers, cap)) for g in range(PEERS)
    ]
    found = []
    for f in range(faces // LANES):
        slot = jnp.broadcast_to(ghost[:, f * LANES : (f + 1) * LANES], (2 * layers, LANES))
        low = jnp.bitwise_and(slot, LANES - 1)
        value = jnp.broadcast_to(other[:, f * LANES : (f + 1) * LANES], (2 * layers, LANES))
        for g in range(PEERS):
            picked = jnp.take_along_axis(table[g], low, axis=1, mode="promise_in_bounds")
            inside = jnp.logical_and(slot >= g * cap, slot < (g + 1) * cap)
            value = jnp.where(inside, picked, value)
        found.append(value[0:1])
    far = jnp.concatenate(found, axis=1)
    where_ref[0] = twice(owner, held)
    where_ref[1] = twice(far, mine)
    cell = lax.broadcasted_iota(jnp.int32, (cells, faces), 0)
    used = slope[layers : layers + 1, :] != 0.0
    one = jnp.float32(1.0)
    hot_ref[0] = jnp.where(cell == owner, one, 0.0).astype(jnp.bfloat16)
    hot_ref[1] = jnp.where(cell == other, one, 0.0).astype(jnp.bfloat16)
    hot_ref[2] = jnp.where(cell == jnp.where(used, mine, -1), one, 0.0).astype(jnp.bfloat16)


def gather_jump(pieces, where_ref, layers, tiles, variables, f):
    rows = 2 * layers
    upper = lax.broadcasted_iota(jnp.int32, (rows, LANES), 0) < layers
    near = where_ref[0, :, f * LANES : (f + 1) * LANES]
    far = where_ref[1, :, f * LANES : (f + 1) * LANES]
    near_low, near_tile = jnp.bitwise_and(near, LANES - 1), lax.shift_right_logical(near, 7)
    far_low, far_tile = jnp.bitwise_and(far, LANES - 1), lax.shift_right_logical(far, 7)
    holder = PIECE_OF_HOLDER[f]

    def take(source, index):
        return jnp.take_along_axis(source, index, axis=1, mode="promise_in_bounds")

    jumps = []
    for v in range(variables):
        value = None
        for t in range(tiles):
            source = jnp.where(upper, pieces[0][v][t], pieces[holder][v][t])
            got = take(source, near_low)
            value = got if value is None else jnp.where(near_tile == t, got, value)
        other = None
        for p in range(len(pieces)):
            for t in range(tiles):
                got = take(pieces[p][v][t], far_low)
                other = got if other is None else jnp.where(far_tile == p * tiles + t, got, other)
        jumps.append(value - other)
    return jumps


def doubled(refs, layers, tiles, variables):
    rows = layers * tiles
    pieces = []
    for ref, base in refs:
        piece = []
        for v in range(variables):
            parts = []
            for t in range(tiles):
                start = base + v * rows + t * layers
                part = ref[start : start + layers, :]
                parts.append(jnp.concatenate([part, part], axis=0))
            piece.append(parts)
        pieces.append(piece)
    return pieces


def side_flux(coefs, nx, ny, e):
    ux, uy, uz, enthalpy, normal, kinetic = coefs
    alpha = ux * e[1] + uy * e[2] + uz * e[3] + enthalpy * e[4]
    beta = (GAMMA - 1.0) * (nx * e[1] + ny * e[2] + normal * e[4])
    total = e[0] + alpha
    return [
        beta * kinetic - alpha * normal,
        nx * total + normal * e[1] - beta * ux,
        ny * total + normal * e[2] - beta * uy,
        normal * e[3] - beta * uz,
        beta + normal * e[4],
    ]


def scatter(value, hot_ref, k):
    got = lax.dot_general(split_rows(value), hot_ref[k], NT, preferred_element_type=jnp.float32)
    half = got.shape[0] // 2
    return got[:half] + got[half:]


def to_tiles(value, tiles):
    return jnp.concatenate([value[:, t * LANES : (t + 1) * LANES] for t in range(tiles)], axis=0)


def state_kernel(layers, tiles, variables, bases, x_ref, a_ref, b_ref, c_ref, flux_ref, where_ref,
                 hot_ref, limiter_ref, p_ref, s_ref, left_ref, right_ref):
    rows = layers * tiles
    size = variables * rows
    refs = ((x_ref, bases[0]), (a_ref, bases[1]), (b_ref, bases[2]), (b_ref, bases[2] + size), (c_ref, bases[3]))
    pieces = doubled(refs, layers, tiles, variables)
    faces = flux_ref.shape[2]
    for f in range(faces // LANES):
        lanes = slice(f * LANES, (f + 1) * LANES)
        e = gather_jump(pieces, where_ref, layers, tiles, variables, f)
        coefs = [flux_ref[k, :, lanes] for k in range(15)]
        bound, nx, ny = coefs[12:]
        left = side_flux(coefs[0:6], nx, ny, e)
        right = side_flux(coefs[6:12], nx, ny, e)
        for v in range(variables):
            left_ref[v * 2 * layers : (v + 1) * 2 * layers, lanes] = left[v] + bound * e[v]
            right_ref[v * 2 * layers : (v + 1) * 2 * layers, lanes] = right[v] - bound * e[v]
    left, right = left_ref[...], right_ref[...]
    near = scatter(left, hot_ref, 0) + scatter(right, hot_ref, 1)
    cut = scatter(right, hot_ref, 2)
    for v in range(variables):
        at = v * 2 * layers
        part = to_tiles(near[at : at + layers] + cut[at + layers : at + 2 * layers], tiles)
        p_ref[v * rows : (v + 1) * rows, :] = part
        s_ref[v * rows : (v + 1) * rows, :] = part * limiter_ref[v * rows : (v + 1) * rows, :]


def slope_kernel(layers, tiles, variables, vectors, with_gram, x_ref, a_ref, b_ref, c_ref, flux_ref,
                 where_ref, hot_ref, p_ref, v_ref, low_ref, high_ref, diag_ref, couple_ref, krylov_ref, *rest):
    finished = rest[:vectors]
    rest = rest[vectors:]
    if with_gram:
        gram_ref, *rest = rest
    w_ref, dots_ref, moved_ref, sums_ref = rest
    rows = layers * tiles
    size = variables * rows
    refs = ((x_ref, 0), (a_ref, 0), (b_ref, 0), (b_ref, size), (c_ref, 0))
    pieces = doubled(refs, layers, tiles, variables)
    faces = flux_ref.shape[2]
    for f in range(faces // LANES):
        lanes = slice(f * LANES, (f + 1) * LANES)
        e = gather_jump(pieces, where_ref, layers, tiles, variables, f)
        slope = flux_ref[15, :, lanes]
        for v in range(variables):
            moved_ref[v * 2 * layers : (v + 1) * 2 * layers, lanes] = slope * e[v]
    moved = moved_ref[...]
    own = scatter(moved, hot_ref, 1) - scatter(moved, hot_ref, 0)
    cut = scatter(moved, hot_ref, 2)
    layer = lax.broadcasted_iota(jnp.int32, (rows, LANES), 0) % layers
    total = []
    for v in range(variables):
        at = v * 2 * layers
        part = slice(v * rows, (v + 1) * rows)
        slope_part = to_tiles(own[at : at + layers] + cut[at + layers : at + 2 * layers], tiles)
        value = v_ref[part, :]
        low = pltpu.roll(low_ref[part, :], rows - (layers - 1), axis=0)
        high = pltpu.roll(high_ref[part, :], layers - 1, axis=0)
        above = jnp.where(layer == layers - 1, high, pltpu.roll(value, rows - 1, axis=0))
        below = jnp.where(layer == 0, low, pltpu.roll(value, 1, axis=0))
        out = diag_ref[...] * value + couple_ref[...] * (2.0 * value - above - below)
        out = out + p_ref[part, :] + slope_part
        w_ref[part, :] = out
        total.append(out)
    sums_ref[...] = jnp.zeros_like(sums_ref)
    basis = krylov_ref.shape[0] // size

    def put(at, ref, base):
        acc = None
        for v in range(variables):
            term = ref[base + v * rows : base + (v + 1) * rows, :] * total[v]
            acc = term if acc is None else acc + term
        sums_ref[at : at + 1, :] = jnp.sum(acc, axis=0, keepdims=True)

    for i in range(basis):
        put(i, krylov_ref, i * size)
    for j in range(vectors):
        put(basis + j, finished[j], 0)
    put(basis + PRODUCTS, w_ref, 0)
    dots = lax.dot_general(
        jnp.ones((8, LANES), jnp.float32), sums_ref[...], NT,
        precision=lax.Precision.HIGHEST, preferred_element_type=jnp.float32,
    )
    if with_gram:
        message = gram_ref[...]
        message = jnp.concatenate([message[0:1] + dots[0:1], message[1:]], axis=0)
        dots_ref[...] = jnp.broadcast_to(message[None], dots_ref.shape)
    else:
        dots_ref[...] = jnp.broadcast_to(dots[0:1], dots_ref.shape)


def inverse_of(packed, basis, per_row, scratch_ref):
    height = scratch_ref.shape[0]
    lane = lax.broadcasted_iota(jnp.int32, (height, LANES), 1)
    row = lax.broadcasted_iota(jnp.int32, (height, LANES), 0)
    scratch_ref[...] = jnp.zeros_like(scratch_ref)
    for i in range(basis):
        at = DOT_LANES + (i % per_row) * basis
        scratch_ref[i : i + 1, 0:basis] = packed[i // per_row : i // per_row + 1, at : at + basis]
    work = scratch_ref[...] + jnp.where(jnp.logical_and(lane == row + basis, row < basis), 1.0, 0.0)
    for k in range(basis):
        pivot_row = work[k : k + 1, :]
        scaled = pivot_row / pivot_row[:, k : k + 1]
        column = jnp.where(row == k, 0.0, jnp.broadcast_to(work[:, k : k + 1], work.shape))
        work = jnp.where(row == k, scaled, work - column * scaled)
    moved = pltpu.roll(work, LANES - basis, axis=1)
    return jnp.where(lane < basis, moved, 0.0)


def update_kernel(count_all, size, vectors, with_gram, per_row, got_ref, w_ref, krylov_ref, *rest):
    finished = rest[:vectors]
    rest = rest[vectors:]
    if with_gram:
        next_ref, hess_ref, inverse_ref, scratch_ref = rest
    else:
        inverse_ref, next_ref, hess_ref = rest
    basis = krylov_ref.shape[0] // size
    scale = 1.0 / count_all
    if with_gram:
        packed = jnp.sum(got_ref[...], axis=0) * scale
        inverse = inverse_of(packed, basis, per_row, scratch_ref)
        inverse_ref[...] = inverse
        p = packed[0:1, :]
    else:
        p = jnp.sum(got_ref[...], axis=0, keepdims=True) * scale
        inverse = inverse_ref[...]
    lane = lax.broadcasted_iota(jnp.int32, (1, LANES), 1)
    square = jnp.sum(jnp.where(lane == basis + PRODUCTS, p, 0.0), axis=1, keepdims=True)
    wide = inverse.shape
    solved = jnp.broadcast_to(jnp.sum(inverse * p, axis=1, keepdims=True), wide)
    diagonal = lax.broadcasted_iota(jnp.int32, wide, 0) == lax.broadcasted_iota(jnp.int32, wide, 1)
    solved_row = jnp.sum(jnp.where(diagonal, solved, 0.0), axis=0, keepdims=True)
    column = jnp.where(lane < basis, solved_row, jnp.where(lane < basis + vectors, p, 0.0))
    norm = jnp.sqrt(square - jnp.sum(column * p, axis=1, keepdims=True) + EPSILON)
    hess_ref[...] = jnp.where(lane == basis + PRODUCTS - 1, norm, column)
    rest_of = w_ref[...]
    for i in range(basis):
        rest_of = rest_of - solved[i : i + 1, :] * krylov_ref[i * size : (i + 1) * size, :]
    for j in range(vectors):
        rest_of = rest_of - p[:, basis + j : basis + j + 1] * finished[j][...]
    next_ref[...] = rest_of / norm


def on_device(krylov, limiter, pseudo_diag, face_states, face_angle, face_area, slope_weight,
              span_coupling, face_cells, send_list, send_count):
    basis, variables, layers, cells = krylov.shape
    cap = send_list.shape[1]
    faces = face_cells.shape[1]
    tiles = cells // LANES
    rows = layers * tiles
    size = variables * rows
    dom_count = lax.axis_size("dom")
    span_count = lax.axis_size("span")
    devices = dom_count * span_count
    count_all = variables * layers * cells * devices
    bits = (cells - 1).bit_length()
    messages = 5 * layers + 4
    height = -(-basis // 8) * 8
    per_row = (LANES - DOT_LANES) // basis
    packed_rows = -(-basis // per_row)

    def in_rows(value):
        lead = value.shape[:-2]
        value = value.reshape(lead + (layers, tiles, LANES))
        return jnp.swapaxes(value, -3, -2).reshape(lead[:-1] + (-1, LANES) if lead else (rows, LANES))

    swap = [(i, i ^ 1) for i in range(dom_count)]
    hop = [(i, i + 2 if i + 2 < dom_count else i + 1) for i in range(0, dom_count, 2)]
    hop += [(i, i - 2 if i >= 2 else i - 1) for i in range(1, dom_count, 2)]
    place = lax.axis_index("dom")
    outside = jnp.logical_or(place == 0, place == dom_count - 1)

    def window(x):
        a = lax.ppermute(x, "dom", swap)
        b = lax.ppermute(jnp.concatenate([x, a], axis=0), "dom", hop)
        c = lax.ppermute(b[size:], "dom", swap)
        return a, b, c

    def layer_neighbours(x):
        up = [(i, (i + 1) % span_count) for i in range(span_count)]
        low = lax.ppermute(x, "span", up)
        if span_count == 2:
            return low, low
        return low, lax.ppermute(x, "span", [(t, s) for s, t in up])

    odd = (lax.axis_index("dom") % 2).astype(jnp.int32).reshape(1)
    as_row = lambda value: value.reshape(1, faces)
    coef, row, index, message = call(
        functools.partial(prepare_kernel, cells, cap, bits),
        (f32(9, layers, faces), f32(3, faces), i32(3, faces), f32(PEERS * messages, cap)),
        odd, face_states, as_row(jnp.cos(face_angle)), as_row(jnp.sin(face_angle)),
        as_row(face_area), as_row(slope_weight), face_cells, send_list, smem=(0,),
    )
    basis_rows = in_rows(krylov.reshape(basis * variables, layers, cells)).reshape(basis * size, LANES)
    current = basis_rows[(basis - 1) * size :]
    first = jnp.concatenate([current, message[messages:]], axis=0)
    a = lax.ppermute(first, "dom", swap)
    second = jnp.concatenate(
        [current, a[:size], message[:messages], a[size + messages :]], axis=0
    )
    b = lax.ppermute(second, "dom", hop)
    got_messages = jnp.where(outside, 0.0, b[2 * size :])
    third = jnp.concatenate([b[size : 2 * size], got_messages[2 * messages :]], axis=0)
    c = lax.ppermute(third, "dom", swap)
    window_now = (a, b, c)

    flux, where, hot = call(
        functools.partial(build_kernel, cells, cap, bits, layers),
        (
            f32(16, 2 * layers, faces),
            i32(2, 2 * layers, faces),
            jax.ShapeDtypeStruct((3, cells, faces), jnp.bfloat16),
        ),
        coef, row, index,
        got_messages[:messages],
        got_messages[messages : 2 * messages],
        a[size : size + messages],
        c[size:],
    )

    gram = jnp.einsum("kvlc,jvlc->kj", krylov, krylov, precision=lax.Precision.HIGHEST)
    gram = jnp.pad(gram, ((0, packed_rows * per_row - basis), (0, 0)))
    gram = gram.reshape(packed_rows, per_row * basis)
    gram = jnp.pad(gram, ((0, 0), (DOT_LANES, LANES - DOT_LANES - per_row * basis)))
    limit_rows = in_rows(limiter)
    diag_rows = in_rows(pseudo_diag)
    couple_rows = jnp.repeat(span_coupling.reshape(tiles, LANES), layers, axis=0)

    vectors = []
    hess_rows = []
    inverse = None
    for number in range(PRODUCTS):
        low, high = layer_neighbours(current)
        state_part, slope_adj = call(
            functools.partial(state_kernel, layers, tiles, variables, (0, 0, 0, 0)),
            (f32(size, LANES), f32(size, LANES)),
            current, *window_now, flux, where, hot, limit_rows,
            scratch=[pltpu.VMEM((variables * 2 * layers, faces), jnp.float32)] * 2,
        )
        slope_window = window(slope_adj)
        with_gram = number == 0
        extra = [gram] if with_gram else []
        dots_shape = f32(devices, packed_rows, LANES) if with_gram else f32(devices, LANES)
        product, dots = call(
            functools.partial(slope_kernel, layers, tiles, variables, number, with_gram),
            (f32(size, LANES), dots_shape),
            slope_adj, *slope_window, flux, where, hot, state_part, current, low, high, diag_rows,
            couple_rows, basis_rows, *vectors, *extra,
            scratch=[
                pltpu.VMEM((variables * 2 * layers, faces), jnp.float32),
                pltpu.VMEM((LANES, LANES), jnp.float32),
            ],
        )
        got = lax.all_to_all(dots, ("span", "dom"), 0, 0, tiled=True)
        next_shapes = (f32(size, LANES), f32(1, LANES))
        update = functools.partial(update_kernel, count_all, size, number, with_gram, per_row)
        if with_gram:
            current, hess, inverse = call(
                update, next_shapes + (f32(height, LANES),), got, product, basis_rows,
                scratch=[pltpu.VMEM((height, LANES), jnp.float32)],
            )
        else:
            current, hess = call(update, next_shapes, got, product, basis_rows, *vectors, inverse)
        vectors.append(current)
        hess_rows.append(hess[:, : basis + PRODUCTS])
        if number + 1 < PRODUCTS:
            window_now = window(current)
    stacked = jnp.stack(vectors).reshape(PRODUCTS, variables, tiles, layers, LANES)
    stacked = jnp.swapaxes(stacked, 2, 3).reshape(PRODUCTS, variables, layers, cells)
    return (stacked, jnp.concatenate(hess_rows, axis=0))


def solution(mesh):
    return jax.shard_map(
        on_device,
        mesh=mesh,
        in_specs=(
            P(None, None, "span", "dom"),
            P(None, "span", "dom"),
            P("span", "dom"),
            P(None, None, "span", "dom"),
            P("dom"),
            P("dom"),
            P("dom"),
            P("dom"),
            P(None, "dom"),
            P(None, "dom"),
            P(None, "dom"),
        ),
        out_specs=(P(None, None, "span", "dom"), P()),
        check_vma=False,
    )
```

```python
import functools

import jax
import jax.numpy as jnp
from jax import lax
from jax.experimental import pallas as pl
from jax.experimental.pallas import tpu as pltpu
from jax.sharding import PartitionSpec as P

PRODUCTS = 3
PEERS = 4
EPSILON = 1e-06
GAMMA = 1.4
LANES = 128
DOT_LANES = 28

SENT_FACES = (((0, 0), (1, 1), (1, 0)), ((1, 3), (0, 2), (0, 3)))
SENT_LISTS = (((1, 3), (1, 2), (0, 3)), ((0, 0), (0, 1), (1, 0)))
HOLDER_BLOCK = ((0, 1, 1), (1, 0, 0))
NAMED_LIST = (((1, 3), (1, 2), (0, 3)), ((0, 0), (0, 1), (1, 0)))
GHOSTS = (
    ((1, 1, 0), (0, 1, None), (2, 0, 1), (2, 1, 2)),
    ((1, 0, 2), (1, 1, 1), (0, 0, None), (2, 0, 0)),
)
NAMING = (((0, 2), (1, 0), (1, 1)), ((0, 0), (0, 1), (1, 2)))

VMEM_LIMIT = 16 * 1024 * 1024
NT = (((1,), (1,)), ((), ()))


def call(kernel, out_shape, *args, smem=(), scratch=()):
    specs = [
        pl.BlockSpec(memory_space=pltpu.SMEM if i in smem else pltpu.VMEM)
        for i in range(len(args))
    ]
    out_specs = jax.tree.map(lambda _: pl.BlockSpec(memory_space=pltpu.VMEM), out_shape)
    return pl.pallas_call(
        kernel,
        out_shape=out_shape,
        in_specs=specs,
        out_specs=out_specs,
        scratch_shapes=list(scratch),
        compiler_params=pltpu.CompilerParams(vmem_limit_bytes=VMEM_LIMIT),
    )(*args)


def f32(*shape):
    return jax.ShapeDtypeStruct(shape, jnp.float32)


def i32(*shape):
    return jax.ShapeDtypeStruct(shape, jnp.int32)


def rows_of(shape):
    return lax.broadcasted_iota(jnp.int32, shape, 0)


def split_rows(value):
    high = value.astype(jnp.bfloat16).astype(jnp.float32)
    return jnp.concatenate([high, value - high], axis=0).astype(jnp.bfloat16)


def pair_swap(value, half):
    count = value.shape[0]
    first = (rows_of(value.shape) // half) % 2 == 0
    return jnp.where(first, pltpu.roll(value, count - half, axis=0), pltpu.roll(value, half, axis=0))


def mix(own, got, role, half):
    mine = (rows_of(own.shape) // half) % 2 == role
    return jnp.where(mine, own, pair_swap(got, half))


def take(source, index):
    return jnp.take_along_axis(source, index, axis=1, mode="promise_in_bounds")


def primitives(states, nx, ny):
    rho, mx, my, mz, energy = states
    inverse = 1.0 / rho
    ux, uy, uz = mx * inverse, my * inverse, mz * inverse
    pressure = (GAMMA - 1.0) * (energy - 0.5 * rho * (ux * ux + uy * uy + uz * uz))
    enthalpy = (energy + pressure) * inverse
    speed = jnp.abs(ux * nx + uy * ny) + jnp.sqrt(GAMMA * pressure * inverse)
    return [ux, uy, uz, enthalpy], speed


def side_terms(prims, nx, ny):
    ux, uy, uz, enthalpy = prims
    return [ux, uy, uz, enthalpy, ux * nx + uy * ny, 0.5 * (ux * ux + uy * uy + uz * uz)]


def spread(rows, each):
    return jnp.concatenate(
        [jnp.broadcast_to(rows[q : q + 1], (each, LANES)) for q in range(rows.shape[0])], axis=0
    )


def prepare_kernel(dims, at, place_ref, raw_ref, got_ref, flux_ref, index_ref, send_a_ref, send_b_ref,
                   value_ref, partner_ref, limiter_ref, diag_ref, couple_ref, pack_ref):
    cells, cap, bits, half, groups, size, variables, message = dims
    role, mirrored = place_ref[0], place_ref[1] == 1

    def own(name):
        start, count = at[name]
        return raw_ref[start : start + count, :], got_ref[start : start + count, :]

    def blocks(start, count):
        mine, other = raw_ref[start : start + count, :], got_ref[start : start + count, :]
        return jnp.where(role == 0, mine, other), jnp.where(role == 0, other, mine)

    mine, other = own("value")
    value = mix(mine, other, role, half)
    value_ref[...] = value
    partner_ref[...] = mix(other, mine, 1 - role, half)
    limiter_ref[...] = mix(*own("limiter"), role, half)
    diag_ref[...] = mix(*own("diag"), role, half)
    couple = blocks(*at["couple"])
    for t in range(cells // LANES):
        for b in range(2):
            row = (2 * t + b) * half
            couple_ref[row : row + half, :] = jnp.broadcast_to(couple[b][t : t + 1], (half, LANES))

    names = ("nx", "ny", "area", "slope", "owner", "other", "lists")
    plane = {name: blocks(*at[name]) for name in names}
    start = at["states"][0]
    picked, lists = [], []
    for b in range(2):
        states = []
        for k in range(2 * variables):
            both = blocks(start + k * groups * 2 * half, groups * 2 * half)[b]
            low = jnp.concatenate([both[2 * half * q : 2 * half * q + half] for q in range(groups)], axis=0)
            high = jnp.concatenate(
                [both[2 * half * q + half : 2 * half * (q + 1)] for q in range(groups)], axis=0
            )
            states.append(jnp.where(role == 0, low, high))
        nx, ny = spread(plane["nx"][b], half), spread(plane["ny"][b], half)
        scale = spread(0.5 * plane["area"][b], half)
        slope = spread(plane["slope"][b], half)
        left, speed_left = primitives(states[:variables], nx, ny)
        right, speed_right = primitives(states[variables:], nx, ny)
        bound = scale * jnp.maximum(speed_left, speed_right)
        nx, ny = nx * scale, ny * scale
        for k, term in enumerate(side_terms(left, nx, ny) + side_terms(right, nx, ny) + [bound, nx, ny, slope]):
            flux_ref[k, b] = term
        pack_ref[...] = jnp.zeros_like(pack_ref)
        for q in range(groups):
            lanes = slice(q * LANES, (q + 1) * LANES)
            for k, term in enumerate(right + [bound]):
                pack_ref[k * half : (k + 1) * half, lanes] = term[q * half : (q + 1) * half]
            scaled = 0.5 * plane["area"][b][q : q + 1]
            tail = [plane["nx"][b][q : q + 1] * scaled, plane["ny"][b][q : q + 1] * scaled]
            tail += [plane["slope"][b][q : q + 1], plane["owner"][b][q : q + 1]]
            for k, term in enumerate(tail):
                row = 5 * half + k
                pack_ref[row : row + 1, lanes] = term

        def line(rows):
            return jnp.concatenate([rows[q : q + 1] for q in range(rows.shape[0])], axis=1)

        owner = line(plane["owner"][b]).astype(jnp.int32)
        ghost = line(plane["other"][b]).astype(jnp.int32) - cells
        group = jnp.zeros_like(ghost)
        for g in range(1, PEERS):
            group = group + (ghost >= g * cap).astype(jnp.int32)
        flipped = ghost + (PEERS - 1 - 2 * group) * cap
        slot = jnp.where(jnp.logical_and(mirrored, ghost >= 0), flipped, ghost)
        plain = plane["lists"][b]
        turned = jnp.concatenate([plain[PEERS - 1 - g : PEERS - g] for g in range(PEERS)], axis=0)
        ordered = jnp.where(mirrored, turned, plain)
        lists.append(ordered)
        index_ref[3 * b : 3 * b + 1, :] = owner
        index_ref[3 * b + 1 : 3 * b + 2, :] = slot + cells
        index_ref[3 * b + 2 : 3 * b + 3, :] = line(ordered).astype(jnp.int32)
        faces = slot.shape[1]
        named = rows_of((PEERS * cap, faces)) == slot
        packed = pack_ref[...]
        result = lax.dot_general(
            split_rows(packed), named.astype(jnp.float32).astype(jnp.bfloat16), NT,
            preferred_element_type=jnp.float32,
        )
        picked.append(result[: packed.shape[0]] + result[packed.shape[0] :])
    for side, ref in enumerate((send_a_ref, send_b_ref)):
        ref[0:size, :] = value
        for g in range(3):
            b, j = SENT_FACES[side][g]
            part = picked[b][0:message, j * cap : (j + 1) * cap]
            b, j = SENT_LISTS[side][g]
            code = part[message - 1 :] * float(1 << bits) + lists[b][j : j + 1]
            row = size + g * message
            ref[row : row + message - 1, :] = part[: message - 1]
            ref[row + message - 1 : row + message, :] = code
        row = size + 3 * message
        ref[row:, :] = jnp.zeros((ref.shape[0] - row, LANES), jnp.float32)


def list_of(index_ref, b, j, cap):
    return index_ref[3 * b + 2 : 3 * b + 3, j * cap : (j + 1) * cap]


def hot_kernel(cells, cap, index_ref, hot_ref):
    faces = index_ref.shape[1]
    inside = []
    for b in range(2):
        local = index_ref[3 * b + 1 : 3 * b + 2, :]
        here = jnp.where(local < cells, local, -1)
        j = b + 1
        table = jnp.broadcast_to(list_of(index_ref, 1 - b, j, cap), (8, cap))
        parts = []
        for f in range(faces // LANES):
            slot = jnp.broadcast_to(local[:, f * LANES : (f + 1) * LANES], (8, LANES)) - cells - j * cap
            got = take(table, jnp.bitwise_and(slot, LANES - 1))
            ok = jnp.logical_and(slot >= 0, slot < cap)
            parts.append(jnp.where(ok, got, -1)[0:1])
        inside.append((here, jnp.concatenate(parts, axis=1)))
    owners = [index_ref[3 * b : 3 * b + 1, :] for b in range(2)]
    cut = []
    for b in range(2):
        pieces = []
        for side, g in NAMING[b]:
            block, j = NAMED_LIST[side][g]
            pieces.append(list_of(index_ref, block, j, cap))
        cut.append(pieces)
    lines = (
        jnp.concatenate(cut[0] + [owners[0], inside[0][0], inside[1][1]], axis=1),
        jnp.concatenate([inside[0][1], inside[1][0], owners[1]] + cut[1], axis=1),
    )
    for b in range(2):
        width = lines[b].shape[1]
        equal = rows_of((cells, width)) == lines[b]
        hot_ref[b] = jnp.where(equal, jnp.float32(1.0), 0.0).astype(jnp.bfloat16)


def build_kernel(cells, cap, bits, half, groups, message, index_ref, a_ref, b_ref, flux_ref, near_ref, far_ref):
    gots = (a_ref, b_ref)
    tiles = cells // LANES

    def stack(parts):
        count = sum(p.shape[0] for p in parts)
        tail = jnp.zeros((groups * half - count, LANES), parts[0].dtype)
        return jnp.concatenate(list(parts) + [tail], axis=0)

    codes = []
    for side, ref in enumerate(gots):
        def block(k):
            return stack([ref[g * message + k * half : g * message + (k + 1) * half, :] for g in range(3)])

        def line(k):
            row = 5 * half + k
            return stack(
                [jnp.broadcast_to(ref[g * message + row : g * message + row + 1, :], (half, LANES)) for g in range(3)]
            )

        nx, ny, slope = line(0), line(1), line(2)
        terms = side_terms([block(k) for k in range(4)], nx, ny) + [block(4), nx, ny, slope]
        for k, term in enumerate(terms):
            flux_ref[k, side] = term
        code = [ref[(g + 1) * message - 1 : (g + 1) * message, :].astype(jnp.int32) for g in range(3)]
        held = [jnp.broadcast_to(lax.shift_right_logical(c, bits), (half, LANES)) for c in code]
        near_ref[2 + side] = stack(held)
        mine = [
            jnp.broadcast_to(list_of(index_ref, *NAMED_LIST[side][g], cap), (half, LANES)) for g in range(3)
        ]
        far_ref[2 + side] = stack(mine)
        codes.append([jnp.bitwise_and(c, (1 << bits) - 1) for c in code])

    def place(cell, piece, block):
        tile = 2 * lax.shift_right_logical(cell, 7) + (2 * tiles * piece + block)
        return tile * LANES + jnp.bitwise_and(cell, LANES - 1)

    for b in range(2):
        owner = [index_ref[3 * b : 3 * b + 1, q * LANES : (q + 1) * LANES] for q in range(groups)]
        other = [index_ref[3 * b + 1 : 3 * b + 2, q * LANES : (q + 1) * LANES] for q in range(groups)]
        near_ref[b] = spread(jnp.concatenate(owner, axis=0), half)
        local = spread(jnp.concatenate(other, axis=0), half)
        value = place(local, 0, b)
        slot = local - cells
        low = jnp.bitwise_and(slot, LANES - 1)
        for j in range(PEERS):
            piece, block, g = GHOSTS[b][j]
            cell = list_of(index_ref, block, j, cap) if g is None else codes[piece - 1][g]
            table = jnp.broadcast_to(place(cell, piece, block), (groups * half, cap))
            inside = jnp.logical_and(slot >= j * cap, slot < (j + 1) * cap)
            value = jnp.where(inside, take(table, low), value)
        far_ref[b] = value


def tile_copies(refs, half, tiles, variables):
    rows = 2 * tiles * half
    row = rows_of((rows, LANES))
    pieces = []
    for ref in refs:
        piece = []
        for v in range(variables):
            value = ref[v * rows : (v + 1) * rows, :]
            parts = []
            for u in range(2 * tiles):
                part = value if u == 0 else pltpu.roll(value, rows - u * half, axis=0)
                width = half
                while width < rows:
                    part = jnp.where(row % (2 * width) < width, part, pltpu.roll(part, width, axis=0))
                    width *= 2
                parts.append(part)
            piece.append(parts)
        pieces.append(piece)
    return pieces


def jumps_of(pieces, near_ref, far_ref, half, tiles, variables, k):
    near, far = near_ref[k], far_ref[k]
    near_low, near_tile = jnp.bitwise_and(near, LANES - 1), lax.shift_right_logical(near, 7)
    far_low, far_tile = jnp.bitwise_and(far, LANES - 1), lax.shift_right_logical(far, 7)
    group = rows_of(near.shape) // half

    def mixed(piece, v, t, which):
        zero, one = pieces[piece][v][2 * t], pieces[piece][v][2 * t + 1]
        pick = jnp.zeros(near.shape, jnp.bool_)
        for g in range(3):
            if which[g]:
                pick = jnp.logical_or(pick, group == g)
        return jnp.where(pick, one, zero)

    jumps = []
    for v in range(variables):
        first, second = None, None
        for t in range(tiles):
            source = pieces[0][v][2 * t + k] if k < 2 else mixed(k - 1, v, t, HOLDER_BLOCK[k - 2])
            got = take(source, near_low)
            first = got if first is None else jnp.where(near_tile == t, got, first)
        if k < 2:
            for p in range(3):
                for u in range(2 * tiles):
                    got = take(pieces[p][v][u], far_low)
                    tile = 2 * tiles * p + u
                    second = got if second is None else jnp.where(far_tile == tile, got, second)
        else:
            blocks = [named[0] for named in NAMED_LIST[k - 2]]
            for t in range(tiles):
                got = take(mixed(0, v, t, blocks), far_low)
                second = got if second is None else jnp.where(far_tile == t, got, second)
        jumps.append(first - second)
    return jumps


def side_flux(coefs, nx, ny, e):
    ux, uy, uz, enthalpy, normal, kinetic = coefs
    alpha = ux * e[1] + uy * e[2] + uz * e[3] + enthalpy * e[4]
    beta = (GAMMA - 1.0) * (nx * e[1] + ny * e[2] + normal * e[4])
    total = e[0] + alpha
    return [
        beta * kinetic - alpha * normal,
        nx * total + normal * e[1] - beta * ux,
        ny * total + normal * e[2] - beta * uy,
        normal * e[3] - beta * uz,
        beta + normal * e[4],
    ]


def put_faces(terms_ref, base, half, groups, v, value):
    for q in range(groups):
        start = base + q * LANES
        terms_ref[v * half : (v + 1) * half, start : start + LANES] = value[q * half : (q + 1) * half]


def put_cut(terms_ref, cap, faces, half, side, v, value):
    for b in range(2):
        for n, (s, g) in enumerate(NAMING[b]):
            if s == side:
                start = n * cap + b * (3 * cap + 4 * faces)
                terms_ref[v * half : (v + 1) * half, start : start + cap] = value[g * half : (g + 1) * half]


def gathered(terms_ref, hot_ref, half, tiles, variables):
    width = hot_ref.shape[2]
    total = terms_ref.shape[1]
    results = []
    for b in range(2):
        value = terms_ref[:, 0:width] if b == 0 else terms_ref[:, total - width :]
        got = lax.dot_general(split_rows(value), hot_ref[b], NT, preferred_element_type=jnp.float32)
        count = got.shape[0] // 2
        results.append(got[:count] + got[count:])
    out = []
    for v in range(variables):
        parts = [
            results[b][v * half : (v + 1) * half, t * LANES : (t + 1) * LANES]
            for t in range(tiles)
            for b in range(2)
        ]
        out.append(jnp.concatenate(parts, axis=0))
    return out


def clear_tail(terms_ref, used):
    terms_ref[used:, :] = jnp.zeros((terms_ref.shape[0] - used, terms_ref.shape[1]), jnp.float32)


def state_kernel(cap, half, groups, tiles, variables, x_ref, a_ref, b_ref, flux_ref, cut_ref, near_ref, far_ref,
                 hot_ref, limiter_ref, p_ref, s_ref, terms_ref):
    rows = 2 * tiles * half
    faces = groups * LANES
    pieces = tile_copies((x_ref, a_ref, b_ref), half, tiles, variables)
    clear_tail(terms_ref, variables * half)
    for k in range(4):
        e = jumps_of(pieces, near_ref, far_ref, half, tiles, variables, k)
        if k < 2:
            coefs = [flux_ref[i, k] for i in range(15)]
            bound, nx, ny = coefs[12:]
            left = side_flux(coefs[0:6], nx, ny, e)
            right = side_flux(coefs[6:12], nx, ny, e)
            left_base = 3 * cap + (0 if k == 0 else 3 * faces)
            right_base = 3 * cap + (1 + k) * faces
            for v in range(variables):
                put_faces(terms_ref, left_base, half, groups, v, left[v] + bound * e[v])
                put_faces(terms_ref, right_base, half, groups, v, right[v] - bound * e[v])
        else:
            coefs = [cut_ref[i, k - 2] for i in range(9)]
            bound, nx, ny = coefs[6:]
            right = side_flux(coefs[0:6], nx, ny, e)
            for v in range(variables):
                put_cut(terms_ref, cap, faces, half, k - 2, v, right[v] - bound * e[v])
    for v, part in enumerate(gathered(terms_ref, hot_ref, half, tiles, variables)):
        p_ref[v * rows : (v + 1) * rows, :] = part
        s_ref[v * rows : (v + 1) * rows, :] = part * limiter_ref[v * rows : (v + 1) * rows, :]


def slope_kernel(cap, half, groups, tiles, variables, vectors, with_gram, place_ref, x_ref, a_ref, b_ref, flux_ref,
                 cut_ref, near_ref, far_ref, hot_ref, p_ref, v_ref, partner_ref, cross_ref, diag_ref, couple_ref,
                 krylov_ref, *rest):
    finished = rest[:vectors]
    rest = rest[vectors:]
    if with_gram:
        gram_ref, *rest = rest
    w_ref, dots_ref, terms_ref, sums_ref = rest
    rows = 2 * tiles * half
    size = variables * rows
    faces = groups * LANES
    role = place_ref[0]
    pieces = tile_copies((x_ref, a_ref, b_ref), half, tiles, variables)
    clear_tail(terms_ref, variables * half)
    for k in range(4):
        e = jumps_of(pieces, near_ref, far_ref, half, tiles, variables, k)
        if k < 2:
            slope = flux_ref[15, k]
            left_base = 3 * cap + (0 if k == 0 else 3 * faces)
            right_base = 3 * cap + (1 + k) * faces
            for v in range(variables):
                moved = slope * e[v]
                put_faces(terms_ref, left_base, half, groups, v, -moved)
                put_faces(terms_ref, right_base, half, groups, v, moved)
        else:
            slope = cut_ref[9, k - 2]
            for v in range(variables):
                put_cut(terms_ref, cap, faces, half, k - 2, v, slope * e[v])
    slope_parts = gathered(terms_ref, hot_ref, half, tiles, variables)
    layer = rows_of((rows, LANES)) % half
    total = []
    for v in range(variables):
        part = slice(v * rows, (v + 1) * rows)
        value = v_ref[part, :]
        partner, cross = partner_ref[part, :], cross_ref[part, :]
        high = pltpu.roll(jnp.where(role == 0, partner, cross), half - 1, axis=0)
        low = pltpu.roll(jnp.where(role == 0, cross, partner), rows - (half - 1), axis=0)
        above = jnp.where(layer == half - 1, high, pltpu.roll(value, rows - 1, axis=0))
        below = jnp.where(layer == 0, low, pltpu.roll(value, 1, axis=0))
        out = diag_ref[...] * value + couple_ref[...] * (2.0 * value - above - below)
        out = out + p_ref[part, :] + slope_parts[v]
        w_ref[part, :] = out
        total.append(out)
    sums_ref[...] = jnp.zeros_like(sums_ref)
    basis = krylov_ref.shape[0] // size

    def put(at, ref, base):
        acc = None
        for v in range(variables):
            term = ref[base + v * rows : base + (v + 1) * rows, :] * total[v]
            acc = term if acc is None else acc + term
        sums_ref[at : at + 1, :] = jnp.sum(acc, axis=0, keepdims=True)

    for i in range(basis):
        put(i, krylov_ref, i * size)
    for j in range(vectors):
        put(basis + j, finished[j], 0)
    put(basis + PRODUCTS, w_ref, 0)
    dots = lax.dot_general(
        jnp.ones((8, LANES), jnp.float32), sums_ref[...], NT,
        precision=lax.Precision.HIGHEST, preferred_element_type=jnp.float32,
    )
    if with_gram:
        message = gram_ref[...]
        message = jnp.concatenate([message[0:1] + dots[0:1], message[1:]], axis=0)
        dots_ref[...] = jnp.broadcast_to(message[None], dots_ref.shape)
    else:
        dots_ref[...] = jnp.broadcast_to(dots[0:1], dots_ref.shape)


def inverse_of(packed, basis, per_row, scratch_ref):
    height = scratch_ref.shape[0]
    lane = lax.broadcasted_iota(jnp.int32, (height, LANES), 1)
    row = rows_of((height, LANES))
    scratch_ref[...] = jnp.zeros_like(scratch_ref)
    for i in range(basis):
        at = DOT_LANES + (i % per_row) * basis
        scratch_ref[i : i + 1, 0:basis] = packed[i // per_row : i // per_row + 1, at : at + basis]
    work = scratch_ref[...] + jnp.where(jnp.logical_and(lane == row + basis, row < basis), 1.0, 0.0)
    for k in range(basis):
        pivot_row = work[k : k + 1, :]
        scaled = pivot_row / pivot_row[:, k : k + 1]
        column = jnp.where(row == k, 0.0, jnp.broadcast_to(work[:, k : k + 1], work.shape))
        work = jnp.where(row == k, scaled, work - column * scaled)
    moved = pltpu.roll(work, LANES - basis, axis=1)
    return jnp.where(lane < basis, moved, 0.0)


def mix_kernel(half, place_ref, own_ref, got_ref, out_ref):
    role = place_ref[0]
    out_ref[...] = mix(own_ref[...], got_ref[...], role, half)


def update_kernel(count_all, size, vectors, with_gram, per_row, got_ref, w_ref, krylov_ref, *rest):
    finished = rest[:vectors]
    rest = rest[vectors:]
    if with_gram:
        next_ref, hess_ref, inverse_ref, scratch_ref = rest
    else:
        inverse_ref, next_ref, hess_ref = rest
    basis = krylov_ref.shape[0] // size
    scale = 1.0 / count_all
    if with_gram:
        packed = jnp.sum(got_ref[...], axis=0) * scale
        inverse = inverse_of(packed, basis, per_row, scratch_ref)
        inverse_ref[...] = inverse
        p = packed[0:1, :]
    else:
        p = jnp.sum(got_ref[...], axis=0, keepdims=True) * scale
        inverse = inverse_ref[...]
    lane = lax.broadcasted_iota(jnp.int32, (1, LANES), 1)
    square = jnp.sum(jnp.where(lane == basis + PRODUCTS, p, 0.0), axis=1, keepdims=True)
    wide = inverse.shape
    solved = jnp.broadcast_to(jnp.sum(inverse * p, axis=1, keepdims=True), wide)
    diagonal = rows_of(wide) == lax.broadcasted_iota(jnp.int32, wide, 1)
    solved_row = jnp.sum(jnp.where(diagonal, solved, 0.0), axis=0, keepdims=True)
    column = jnp.where(lane < basis, solved_row, jnp.where(lane < basis + vectors, p, 0.0))
    norm = jnp.sqrt(square - jnp.sum(column * p, axis=1, keepdims=True) + EPSILON)
    hess_ref[...] = jnp.where(lane == basis + PRODUCTS - 1, norm, column)
    value = w_ref[...]
    for i in range(basis):
        value = value - solved[i : i + 1, :] * krylov_ref[i * size : (i + 1) * size, :]
    for j in range(vectors):
        value = value - p[:, basis + j : basis + j + 1] * finished[j][...]
    next_ref[...] = value / norm


def output_kernel(half, size, place_ref, *refs):
    out_ref = refs[-1]
    for m in range(PRODUCTS):
        out_ref[m * size : (m + 1) * size, :] = mix(refs[2 * m][...], refs[2 * m + 1][...], place_ref[0], half)


def on_device(krylov, limiter, pseudo_diag, face_states, face_angle, face_area, slope_weight,
              span_coupling, face_cells, send_list, send_count):
    basis, variables, layers, cells = krylov.shape
    cap = send_list.shape[1]
    faces = face_cells.shape[1]
    tiles = cells // LANES
    groups = faces // LANES
    half = layers // 2
    rows = layers * tiles
    size = variables * rows
    dom_count = lax.axis_size("dom")
    span_count = lax.axis_size("span")
    devices = dom_count * span_count
    count_all = variables * layers * cells * devices
    bits = (cells - 1).bit_length()
    message = 5 * half + 4
    height = -(-basis // 8) * 8
    per_row = (LANES - DOT_LANES) // basis
    packed_rows = -(-basis // per_row)

    def in_rows(value):
        width = value.shape[-1] // LANES
        value = value.reshape((-1, layers, width, LANES))
        return jnp.swapaxes(value, 1, 2).reshape(-1, LANES)

    block = lax.axis_index("dom")
    pair = block // 2
    mirrored = pair % 2
    role = (block + mirrored) % 2
    place = jnp.stack([role, mirrored]).astype(jnp.int32)
    at_end = jnp.logical_or(pair == 0, pair == dom_count // 2 - 1)

    swap = [(i, i ^ 1) for i in range(dom_count)]
    to_a = [(i, i ^ 3) for i in range(dom_count)]
    to_b = []
    for i in range(dom_count):
        other = ((i // 2 + 1) ^ 1) - 1
        to_b.append((i, 2 * other + 1 - i % 2 if 0 <= other < dom_count // 2 else i ^ 1))
    cross = []
    for s in range(span_count):
        for i in range(dom_count):
            step = 1 if (i + i // 2) % 2 else -1
            cross.append((s * dom_count + i, ((s + step) % span_count) * dom_count + (i ^ 1)))

    def send(x, pairs):
        return lax.ppermute(x, "dom", pairs)

    def neighbours(x):
        return send(x, to_a), send(x, to_b)

    def across(x):
        return lax.ppermute(x, ("span", "dom"), cross)

    basis_rows = in_rows(krylov)
    parts = {
        "value": basis_rows[(basis - 1) * size :],
        "limiter": in_rows(limiter),
        "diag": in_rows(pseudo_diag),
        "states": in_rows(face_states),
        "nx": jnp.cos(face_angle).reshape(groups, LANES),
        "ny": jnp.sin(face_angle).reshape(groups, LANES),
        "area": face_area.reshape(groups, LANES),
        "slope": slope_weight.reshape(groups, LANES),
        "owner": face_cells[0].astype(jnp.float32).reshape(groups, LANES),
        "other": face_cells[1].astype(jnp.float32).reshape(groups, LANES),
        "lists": send_list.astype(jnp.float32),
        "couple": span_coupling.reshape(tiles, LANES),
    }
    at, start = {}, 0
    for name, value in parts.items():
        at[name] = (start, value.shape[0])
        start += value.shape[0]
    raw = jnp.concatenate(list(parts.values()), axis=0)
    got_raw = send(raw, swap)
    sent_rows = -(-(size + 3 * message) // 8) * 8
    dims = (cells, cap, bits, half, groups, size, variables, message)
    (flux, index, send_a, send_b, current, partner, limit_rows, diag_rows, couple_rows) = call(
        functools.partial(prepare_kernel, dims, at),
        (
            f32(16, 2, groups * half, LANES), i32(6, faces), f32(sent_rows, LANES), f32(sent_rows, LANES),
            f32(size, LANES), f32(size, LANES), f32(size, LANES), f32(rows, LANES), f32(rows, LANES),
        ),
        place, raw, got_raw, smem=(0,),
        scratch=[pltpu.VMEM((-(-message // 8) * 8, faces), jnp.float32)],
    )
    got_a = send(send_a, to_a)
    got_b = send(send_b, to_b)
    message_b = jnp.where(at_end, 0.0, got_b[size:])
    hot_width = 3 * cap + 3 * faces
    hot = call(
        functools.partial(hot_kernel, cells, cap),
        jax.ShapeDtypeStruct((2, cells, hot_width), jnp.bfloat16),
        index,
    )
    cut, near, far = call(
        functools.partial(build_kernel, cells, cap, bits, half, groups, message),
        (
            f32(10, 2, groups * half, LANES), i32(4, groups * half, LANES), i32(4, groups * half, LANES),
        ),
        index, got_a[size:], message_b,
    )
    window = (got_a[:size], got_b[:size])

    mixed_rows = call(
        functools.partial(mix_kernel, half), f32(basis * size, LANES), place, basis_rows, send(basis_rows, swap),
        smem=(0,),
    )

    gram = jnp.einsum("kvlc,jvlc->kj", krylov, krylov, precision=lax.Precision.HIGHEST)
    gram = jnp.pad(gram, ((0, packed_rows * per_row - basis), (0, 0)))
    gram = gram.reshape(packed_rows, per_row * basis)
    gram = jnp.pad(gram, ((0, 0), (DOT_LANES, LANES - DOT_LANES - per_row * basis)))

    terms = pltpu.VMEM((-(-variables * half // 8) * 8, 6 * cap + 4 * faces), jnp.float32)
    vectors = []
    finished = []
    hess_rows = []
    inverse = None
    for number in range(PRODUCTS):
        crossed = across(current)
        state_part, slope_adj = call(
            functools.partial(state_kernel, cap, half, groups, tiles, variables),
            (f32(size, LANES), f32(size, LANES)),
            current, *window, flux, cut, near, far, hot, limit_rows,
            scratch=[terms],
        )
        slope_window = neighbours(slope_adj)
        with_gram = number == 0
        extra = [gram] if with_gram else []
        dots_shape = f32(devices, packed_rows, LANES) if with_gram else f32(devices, LANES)
        product, dots = call(
            functools.partial(slope_kernel, cap, half, groups, tiles, variables, number, with_gram),
            (f32(size, LANES), dots_shape),
            place, slope_adj, *slope_window, flux, cut, near, far, hot, state_part, current, partner, crossed,
            diag_rows, couple_rows, mixed_rows, *vectors, *extra,
            smem=(0,),
            scratch=[terms, pltpu.VMEM((LANES, LANES), jnp.float32)],
        )
        got = lax.all_to_all(dots, ("span", "dom"), 0, 0, tiled=True)
        shapes = (f32(size, LANES), f32(1, LANES))
        update = functools.partial(update_kernel, count_all, size, number, with_gram, per_row)
        if with_gram:
            current, hess, inverse = call(
                update, shapes + (f32(height, LANES),), got, product, mixed_rows,
                scratch=[pltpu.VMEM((height, LANES), jnp.float32)],
            )
        else:
            current, hess = call(update, shapes, got, product, mixed_rows, *vectors, inverse)
        hess_rows.append(hess[:, : basis + PRODUCTS])
        vectors.append(current)
        if number + 1 < PRODUCTS:
            window = neighbours(current)
        partner = send(current, swap)
        finished += [current, partner]
    stacked = call(
        functools.partial(output_kernel, half, size), f32(PRODUCTS * size, LANES), place, *finished, smem=(0,)
    )
    stacked = stacked.reshape(PRODUCTS, variables, tiles, layers, LANES)
    stacked = jnp.swapaxes(stacked, 2, 3).reshape(PRODUCTS, variables, layers, cells)
    return (stacked, jnp.concatenate(hess_rows, axis=0))


def solution(mesh):
    return jax.shard_map(
        on_device,
        mesh=mesh,
        in_specs=(
            P(None, None, "span", "dom"),
            P(None, "span", "dom"),
            P("span", "dom"),
            P(None, None, "span", "dom"),
            P("dom"),
            P("dom"),
            P("dom"),
            P("dom"),
            P(None, "dom"),
            P(None, "dom"),
            P(None, "dom"),
        ),
        out_specs=(P(None, None, "span", "dom"), P()),
        check_vma=False,
    )
```
